32 devices in a mesh: dp: 8 (over y, x, core), tensor: 4 (over z).
Axes of the slice: x: 2, y: 2, z: 4, core: 2. Of those that a mesh axis runs over, the one named last changes fastest.
Arguments:
- tokens: bfloat16 [12288, 768], P('dp'), may hold values from -6 to 6
- cotangent: bfloat16 [12288, 768], P('dp'), may hold values from -6 to 6
- dealing: int32 [12288], P('dp'), may hold values from 0 to 12287, as said below
- segments: int32 [8, 1536], P('dp'), may hold values from 0 to 7, never falling along the last dimension, each value on 1 to 1024 neighbouring positions
- w_query: float32 [768, 768], P('dp', 'tensor'), may hold values from -0.21875 to 0.21875
- w_key: float32 [768, 768], P('dp', 'tensor'), may hold values from -0.21875 to 0.21875
- w_value: float32 [768, 768], P('dp', 'tensor'), may hold values from -0.21875 to 0.21875
- b_query: float32 [768], P('tensor'), may hold values from -3 to 3
- b_value: float32 [768], P('tensor'), may hold values from -3 to 3
- w_out: float32 [768, 768], P('tensor', 'dp'), may hold values from -0.875 to 0.875
- b_out: float32 [768], replicated, may hold values from -1.75 to 1.75
- gain_one: float32 [768], replicated, may hold values from 0.5 to 1.5
- shift_one: float32 [768], replicated, may hold values from -1.75 to 1.75
- w_up: float32 [768, 3072], P('dp', 'tensor'), may hold values from -0.21875 to 0.21875
- b_up: float32 [3072], P('tensor'), may hold values from -1.75 to 1.75
- w_down: float32 [3072, 768], P('tensor', 'dp'), may hold values from -0.109375 to 0.109375
- b_down: float32 [768], replicated, may hold values from -1.75 to 1.75
- gain_two: float32 [768], replicated, may hold values from 0.5 to 1.5
- shift_two: float32 [768], replicated, may hold values from -1.75 to 1.75
Outputs:
- layer_out: bfloat16 [12288, 768], P('dp')
- grad_tokens: bfloat16 [12288, 768], P('dp')
- query_grad: float32 [768, 768], P('dp', 'tensor')
- key_grad: float32 [768, 768], P('dp', 'tensor')
- value_grad: float32 [768, 768], P('dp', 'tensor')
- qbias_grad: float32 [768], P('tensor')
- vbias_grad: float32 [768], P('tensor')
- out_grad: float32 [768, 768], P('tensor', 'dp')
- obias_grad: float32 [768], replicated
- gain1_grad: float32 [768], replicated
- shift1_grad: float32 [768], replicated
- up_grad: float32 [768, 3072], P('dp', 'tensor')
- ubias_grad: float32 [3072], P('tensor')
- down_grad: float32 [3072, 768], P('tensor', 'dp')
- dbias_grad: float32 [768], replicated
- gain2_grad: float32 [768], replicated
- shift2_grad: float32 [768], replicated
The draws below stay inside these ranges and needn't reach their ends.
Inputs may be any that keep to these rules, and one draw needn't show every extreme that they name: dealing is a permutation of the 12288 given-order tokens; the positions j*1536 to (j+1)*1536 - 1 form group j, and each group takes exactly 192 tokens from each block of 1536 given-order tokens. `segments`: row j gives the sequence of each position of group j: numbers never fall along a row, each sequence has 1 to 1024 positions, one has exactly 1024.
All inputs are finite; a program needn't handle non-finite values.
Results may differ from the reference program's by a relative error of at most 0.014.
The reference program's roundings to bfloat16 on the way count: a program that leaves them out, or rounds other values in their place, can miss the bound.
Values may be sent and summed in bfloat16 or wider, within the bound.
A program may use at most 128 MiB of HBM per device.

```python
import math
import jax
import jax.numpy as jnp
import numpy as np
from jax import lax

D = 768
HEADS = 12
HEAD_DIM = 64
FF = 3072
ROWS = 1536
SEGS = 8
MAXLEN = 1024
TOKENS = 12288
N_DP = 8


def draw_dealing(key, part):
    group_count = TOKENS // ROWS
    per_source = ROWS // group_count
    first_key, second_key = jax.random.split(key)
    local_rows = jax.vmap(lambda one_key: jax.random.permutation(one_key, ROWS))(jax.random.split(first_key, group_count))
    source = local_rows.astype(jnp.int32) + (jnp.arange(group_count, dtype=jnp.int32) * ROWS)[:, None]
    source = source.reshape(group_count, group_count, per_source).transpose(1, 0, 2).reshape(group_count, ROWS)
    shuffle = jax.vmap(lambda one_key: jax.random.permutation(one_key, ROWS))(jax.random.split(second_key, group_count))
    return jnp.take_along_axis(source, shuffle.astype(jnp.int32), axis=1).reshape(TOKENS).astype(jnp.int32)


def steps_of(key, shape, cuts, low, top_value):
    def one(position, shards_of):
        steps = jax.random.uniform(jax.random.fold_in(jax.random.fold_in(key, 6), position), (shards_of,), jnp.float32, low / len(cuts), top_value / len(cuts))
        return jnp.repeat(jnp.exp(steps), shape[position] // shards_of).reshape((-1,) + (1,) * (len(shape) - position - 1))

    level = one(*cuts[0])
    for cut in cuts[1:]:
        level = level * one(*cut)
    return level


def split_up(amount, total, limit, skew):
    portions = [(1 << 20) // math.isqrt(grade ** skew) + 1 for grade in range(2, amount + 1)]
    spare, counts = total - limit - (amount - 1), [1] * (amount - 1)
    while spare > 0:
        candidates = [i for i in range(amount - 1) if counts[i] < limit]
        whole, remaining = sum([portions[i] for i in candidates]), spare
        for i in candidates:
            extra = min(limit - counts[i], max(1, remaining * portions[i] // whole), spare)
            counts[i] = counts[i] + extra
            spare = spare - extra
    return np.array([limit] + counts)


def uneven_parts(rng, amount, total, reach, slope):
    if amount == 2:
        one = jax.random.randint(rng, (), max(1, total - reach), min(reach, total - 1) + 1)
        return jnp.stack([one, total - one])
    tallies = jnp.asarray(split_up(amount, total, reach, slope), jnp.int32)
    twos = (amount - 1) // 2
    giver, receiver = tallies[1:1 + 2 * twos:2], tallies[2:2 + 2 * twos:2]
    margin = jnp.minimum(giver - 1, reach - receiver)
    passed = jax.random.randint(jax.random.fold_in(rng, 1), (twos,), 0, 1 << 20) % (margin + 1)
    tallies = tallies.at[1:1 + 2 * twos:2].set(giver - passed).at[2:2 + 2 * twos:2].set(receiver + passed)
    return tallies[jax.random.permutation(jax.random.fold_in(rng, 2), amount)]


def normal_values(own_key, shape, deviation, bound, pieces=(), held_as=jnp.bfloat16):
    drawn = deviation * jax.random.normal(own_key, shape, jnp.float32)
    if pieces:
        drawn = drawn * steps_of(own_key, shape, pieces, -0.22, 0.18)
    return jnp.clip(drawn, -bound, bound).astype(held_as)


def setup_inputs(seed: int = 0) -> dict:
    streams_of = jax.random.split(jax.random.key(seed), 20)
    return {
        "tokens": normal_values(streams_of[0], (TOKENS, D), 1.0, 6.0, ((0, 8),)),
        "cotangent": normal_values(streams_of[1], (TOKENS, D), 1.0, 6.0, ((0, 8),)),
        "dealing": draw_dealing(jax.random.fold_in(streams_of[19], 71), 0),
        "segments": jax.vmap(lambda own: jnp.searchsorted(jnp.cumsum(uneven_parts(own, SEGS, ROWS, MAXLEN, 2)), jnp.arange(ROWS), side="right"))(jax.random.split(streams_of[3], N_DP)).reshape((N_DP, ROWS)).astype(jnp.int32),
        "w_query": normal_values(streams_of[4], (D, D), D ** -0.5, 0.21875, ((0, 8), (1, 4)), jnp.float32),
        "w_key": normal_values(streams_of[5], (D, D), D ** -0.5, 0.21875, ((0, 8), (1, 4)), jnp.float32),
        "w_value": normal_values(streams_of[6], (D, D), D ** -0.5, 0.21875, ((0, 8), (1, 4)), jnp.float32),
        "b_query": normal_values(streams_of[7], (D,), 0.5, 3.0, ((0, 4),), jnp.float32),
        "b_value": normal_values(streams_of[8], (D,), 0.5, 3.0, ((0, 4),), jnp.float32),
        "w_out": normal_values(streams_of[9], (D, D), (D // 16) ** -0.5, 0.875, ((0, 4), (1, 8)), jnp.float32),
        "b_out": normal_values(streams_of[10], (D,), 0.3, 1.75, (), jnp.float32),
        "gain_one": jnp.clip(1.0 + 0.1 * jax.random.normal(streams_of[11], (D,), jnp.float32), 0.5, 1.5),
        "shift_one": normal_values(streams_of[12], (D,), 0.3, 1.75, (), jnp.float32),
        "w_up": normal_values(streams_of[13], (D, FF), D ** -0.5, 0.21875, ((0, 8), (1, 4)), jnp.float32),
        "b_up": normal_values(streams_of[14], (FF,), 0.3, 1.75, ((0, 4),), jnp.float32),
        "w_down": normal_values(streams_of[15], (FF, D), FF ** -0.5, 0.109375, ((0, 4), (1, 8)), jnp.float32),
        "b_down": normal_values(streams_of[16], (D,), 0.3, 1.75, (), jnp.float32),
        "gain_two": jnp.clip(1.0 + 0.1 * jax.random.normal(streams_of[17], (D,), jnp.float32), 0.5, 1.5),
        "shift_two": normal_values(streams_of[18], (D,), 0.3, 1.75, (), jnp.float32),
    }


EPSILON = 1e-05
PRECISE = lax.Precision.HIGHEST

@jax.custom_vjp
def low(v):
    return lax.optimization_barrier(v.astype(jnp.bfloat16)).astype(jnp.float32)

@jax.custom_vjp
def low_back(v):
    return v

def low_keep(v):
    return (low(v), None)

def low_pass(kept, grad):
    return (grad,)

def back_keep(v):
    return (v, None)

def back_low(kept, grad):
    return (low(grad),)
low.defvjp(low_keep, low_pass)
low_back.defvjp(back_keep, back_low)

def layer_norm(rows_in, gain, shift):
    center = rows_in - lax.optimization_barrier(jnp.mean(rows_in, axis=-1, keepdims=True))
    spread = lax.optimization_barrier(jnp.mean(center * center, axis=-1, keepdims=True))
    return center * lax.rsqrt(spread + EPSILON) * gain + shift

def product(left, right):
    return jnp.dot(left, right, precision=PRECISE, preferred_element_type=jnp.float32)

def group_layer(params, group_in, group_seg):
    query_w, key_w, value_w, b_query, b_value, out_w, b_out, gain_one, shift_one, up_w, b_up, down_w, b_down, gain_two, shift_two = params
    row_count = group_in.shape[0]
    queries = low(low_back((product(group_in, query_w) + b_query) * 0.125)).reshape(row_count, HEADS, HEAD_DIM)
    key_rows = low(low_back(product(group_in, key_w))).reshape(row_count, HEADS, HEAD_DIM)
    value_rows = low(low_back(product(group_in, value_w) + b_value)).reshape(row_count, HEADS, HEAD_DIM)
    scores = low_back(jnp.einsum('qhd,khd->hqk', queries, key_rows, precision=PRECISE))
    same_doc = group_seg[:, None] == group_seg[None, :]
    scores = jnp.where(same_doc[None], scores, -1e+30)
    probs = jax.nn.softmax(scores, axis=-1)
    mixed = jnp.einsum('hqk,khd->qhd', low(probs), value_rows, precision=PRECISE).reshape(row_count, HEADS * HEAD_DIM)
    attn_out = low_back(product(low(low_back(mixed)), out_w) + b_out)
    first_norm = layer_norm(group_in + attn_out, gain_one, shift_one)
    hidden = low(jax.nn.gelu(low_back(product(low(first_norm), up_w) + b_up), approximate=False))
    branch = low_back(product(hidden, down_w) + b_down)
    return layer_norm(first_norm + branch, gain_two, shift_two)

def forward(tokens_f, dealing, segments, query_w, key_w, value_w, b_query, b_value, out_w, b_out, gain_one, shift_one, up_w, b_up, down_w, b_down, gain_two, shift_two):
    params = (low(query_w), low(key_w), low(value_w), b_query, b_value, low(out_w), b_out, gain_one, shift_one, low(up_w), b_up, low(down_w), b_down, gain_two, shift_two)
    group_count = TOKENS // ROWS
    grouped = tokens_f[dealing].reshape(group_count, ROWS, D)
    step_fn = jax.checkpoint(lambda group_in, group_seg: group_layer(params, group_in, group_seg))
    result = lax.map(lambda group_pair: step_fn(group_pair[0], group_pair[1]), (grouped, segments))
    flat = result.reshape(TOKENS, D)
    return jnp.zeros_like(flat).at[dealing].set(flat)

def reference(tokens, cotangent, dealing, segments, w_query, w_key, w_value, b_query, b_value, w_out, b_out, gain_one, shift_one, w_up, b_up, w_down, b_down, gain_two, shift_two):
    tokens_f = tokens.astype(jnp.float32)
    params = (w_query, w_key, w_value, b_query, b_value, w_out, b_out, gain_one, shift_one, w_up, b_up, w_down, b_down, gain_two, shift_two)

    def whole(tok_in, *rest):
        return forward(tok_in, dealing, segments, *rest)
    result, pullback = jax.vjp(whole, tokens_f, *params)
    grads = pullback(cotangent.astype(jnp.float32))
    return (result.astype(jnp.bfloat16), grads[0].astype(jnp.bfloat16), grads[1], grads[2], grads[3], grads[4], grads[5], grads[6], grads[7], grads[8], grads[9], grads[10], grads[11], grads[12], grads[13], grads[14], grads[15])
```

```python
import functools

import jax
import jax.numpy as jnp
from jax import lax
from jax.experimental import pallas as pl
from jax.experimental.pallas import tpu as pltpu
from jax.sharding import PartitionSpec as P

HEAD_DIM = 64
EPSILON = 1e-05
NEGATIVE = -1e30
MESH = pl.DeviceIdType.MESH
F32 = jnp.float32
BF16 = jnp.bfloat16
VMEM_LIMIT = 56 * 1024 * 1024


def vmem_spec():
    return pl.BlockSpec(memory_space=pltpu.VMEM)


def layer_norm(rows_in, gain, shift):
    center = rows_in - jnp.mean(rows_in, axis=-1, keepdims=True)
    spread = jnp.mean(center * center, axis=-1, keepdims=True)
    return center * lax.rsqrt(spread + EPSILON) * gain + shift


def norm_back(rows_in, gain, shift, upstream):
    result, pullback = jax.vjp(layer_norm, rows_in, gain, shift)
    return pullback(upstream)


def exact_gelu(values):
    return jax.nn.gelu(values, approximate=False)


def remote(src, dst, send_sem, recv_sem, device):
    return pltpu.make_async_remote_copy(
        src_ref=src,
        dst_ref=dst,
        send_sem=send_sem,
        recv_sem=recv_sem,
        device_id=device,
        device_id_type=MESH,
    )


def greet(devices):
    barrier = pltpu.get_barrier_semaphore()
    for device in devices:
        pl.semaphore_signal(barrier, inc=1, device_id=device, device_id_type=MESH)
    pl.semaphore_wait(barrier, len(devices))


def comm_call(kernel, out_shape, scratch, cid, args):
    return pl.pallas_call(
        kernel,
        out_shape=out_shape,
        in_specs=[vmem_spec()] * len(args),
        out_specs=[vmem_spec()] * len(out_shape),
        scratch_shapes=scratch,
        compiler_params=pltpu.CompilerParams(
            collective_id=cid, has_side_effects=True, vmem_limit_bytes=VMEM_LIMIT
        ),
    )(*args)


def meta_kernel(nd, nz, meta_ref, bias_ref, meta_out, bias_out, ssem, rsem):
    d, z = lax.axis_index("dp"), lax.axis_index("tensor")
    plane = [{"dp": lax.rem(d + k, nd)} for k in range(1, nd)]
    column = [{"tensor": lax.rem(z + k, nz)} for k in range(1, nz)]
    greet(plane + column)
    copies = []
    for i, device in enumerate(plane):
        copies.append(remote(meta_ref, meta_out.at[d], ssem.at[i], rsem.at[i], device))
    for j, device in enumerate(column):
        i = len(plane) + j
        copies.append(remote(bias_ref, bias_out.at[z], ssem.at[i], rsem.at[i], device))
    for copy in copies:
        copy.start()
    meta_out[d] = meta_ref[...]
    bias_out[z] = bias_ref[...]
    for copy in copies:
        copy.wait()


def index_kernel(nd, gpp, rows, meta_ref, loc_ref, seg_ref):
    per = rows // nd
    d, z = lax.axis_index("dp"), lax.axis_index("tensor")
    group = z * gpp + d // 4
    lane_i = lax.broadcasted_iota(jnp.int32, (128, 128), 0)
    lane_j = lax.broadcasted_iota(jnp.int32, (128, 128), 1)
    upper = (lane_i <= lane_j).astype(F32)
    row_i = lax.broadcasted_iota(jnp.int32, (16, 16), 0)
    row_j = lax.broadcasted_iota(jnp.int32, (16, 16), 1)
    lower = (row_j < row_i).astype(F32)
    rank_of = lax.broadcasted_iota(jnp.int32, (per, 128), 0).astype(F32)

    def pick(deal, source, values):
        low = source * rows
        hit = (deal >= low) & (deal < low + rows)
        ones = jnp.where(hit, 1.0, 0.0)
        inner = jnp.dot(ones, upper, preferred_element_type=F32)
        total = jnp.broadcast_to(inner[:, 127:128], (16, 128))
        before = jnp.dot(lower, total, preferred_element_type=F32)
        key = jnp.where(hit, inner + before - 1.0, -1.0)
        found = jnp.zeros((per, 128), F32)
        for c in range(rows // 128):
            found = found + jnp.where(rank_of == key[c : c + 1, :], values[c : c + 1, :], 0.0)
        return jnp.sum(found, axis=1, keepdims=True).astype(jnp.int32)

    for g in range(nd):
        deal = meta_ref[g, 0:16, :]
        loc_ref[g] = pick(deal, d, (deal - d * rows).astype(F32))
    own_deal = meta_ref[group, 0:16, :]
    own_seg = meta_ref[group, 16:32, :].astype(F32)
    for s in range(nd):
        seg_ref[s] = pick(own_deal, s, own_seg)


def gather_kernel(nd, gpp, rows, loc_ref, tok_ref, cot_ref, tok_out, cot_out):
    per = rows // nd
    z = lax.axis_index("tensor")
    column = lax.broadcasted_iota(jnp.int32, (per, rows), 1)
    for k in range(gpp):
        loc = loc_ref[z * gpp + k]
        pick = jnp.where(column == loc, 1.0, 0.0).astype(BF16)
        tok_out[k] = jnp.dot(pick, tok_ref[...], preferred_element_type=F32).astype(BF16)
        cot_out[k] = jnp.dot(pick, cot_ref[...], preferred_element_type=F32).astype(BF16)


def dispatch_kernel(
    nd, nz, gpp, tok_ref, cot_ref, wqkv_ref, x_out, cot_out, w_out, ssem, rsem, lsem
):
    d, z = lax.axis_index("dp"), lax.axis_index("tensor")
    t = lax.rem(d, 4)
    quarter = nd // 4
    everyone = []
    for kz in range(nz):
        for kd in range(nd):
            if kz or kd:
                everyone.append({"dp": lax.rem(d + kd, nd), "tensor": lax.rem(z + kz, nz)})
    greet(everyone)
    waits = []
    locals_ = []
    for k in range(1, nd):
        dest = lax.rem(d + k, nd)
        copy = remote(tok_ref.at[dest // 4], x_out.at[d], ssem.at[k], rsem.at[k], {"dp": dest})
        copy.start()
        waits.append(copy)
    own = pltpu.make_async_copy(tok_ref.at[d // 4], x_out.at[d], lsem.at[0])
    own.start()
    locals_.append(own)
    base = nd
    for m in range(gpp):
        for kz in range(nz):
            dest = 4 * m + z
            dz = lax.rem(z + kz, nz)
            copy = remote(
                wqkv_ref,
                w_out.at[d],
                ssem.at[base + m * nz + kz],
                rsem.at[base + d],
                {"dp": dest, "tensor": dz},
            )
            if kz == 0:

                @pl.when(dest != d)
                def _():
                    copy.start()

                @pl.when(dest == d)
                def _():
                    pltpu.make_async_copy(wqkv_ref, w_out.at[d], lsem.at[1]).start()
            else:
                copy.start()
    base_c = base + max(nd, gpp * nz)
    for k in range(gpp):
        dest = 4 * k + d // quarter
        copy = remote(
            cot_ref.at[k],
            cot_out.at[lax.rem(d, quarter)],
            ssem.at[base_c + k],
            rsem.at[base_c + lax.rem(d, quarter)],
            {"dp": dest},
        )

        @pl.when(dest != d)
        def _():
            copy.start()

        @pl.when(dest == d)
        def _():
            pltpu.make_async_copy(
                cot_ref.at[k], cot_out.at[lax.rem(d, quarter)], lsem.at[2]
            ).start()

    for copy in waits:
        copy.wait()
    for copy in locals_:
        copy.wait()
    for m in range(gpp):
        for kz in range(nz):
            dest = 4 * m + z
            send = remote(
                wqkv_ref,
                w_out.at[d],
                ssem.at[base + m * nz + kz],
                rsem.at[base + d],
                {"dp": dest, "tensor": lax.rem(z + kz, nz)},
            )
            if kz == 0:

                @pl.when(dest != d)
                def _():
                    send.wait_send()

                @pl.when(dest == d)
                def _():
                    pltpu.make_async_copy(wqkv_ref, w_out.at[d], lsem.at[1]).wait()
            else:
                send.wait_send()
    for s in range(nd):
        came = remote(
            wqkv_ref, w_out.at[s], ssem.at[base], rsem.at[base + s], {"dp": s, "tensor": t}
        )

        @pl.when(jnp.logical_or(t != z, d != s))
        def _():
            came.wait_recv()

    for k in range(gpp):
        dest = 4 * k + d // quarter
        send = remote(
            cot_ref.at[k],
            cot_out.at[lax.rem(d, quarter)],
            ssem.at[base_c + k],
            rsem.at[base_c + lax.rem(d, quarter)],
            {"dp": dest},
        )

        @pl.when(dest != d)
        def _():
            send.wait_send()

        @pl.when(dest == d)
        def _():
            pltpu.make_async_copy(
                cot_ref.at[k], cot_out.at[lax.rem(d, quarter)], lsem.at[2]
            ).wait()

    for j in range(quarter):
        source = t * quarter + j
        came = remote(
            cot_ref.at[0], cot_out.at[j], ssem.at[base_c], rsem.at[base_c + j], {"dp": source}
        )

        @pl.when(source != d)
        def _():
            came.wait_recv()


def quad_kernel(nd, in_ref, out_ref, ssem, rsem):
    d = lax.axis_index("dp")
    t = lax.rem(d, 4)
    first = d - t
    peers = [lax.rem(t + k, 4) for k in range(1, 4)]
    greet([{"dp": first + peer} for peer in peers])
    copies = []
    for i, peer in enumerate(peers):
        copies.append(
            remote(in_ref.at[peer], out_ref.at[t], ssem.at[i], rsem.at[i], {"dp": first + peer})
        )
    for copy in copies:
        copy.start()
    out_ref[t] = in_ref[t]
    for copy in copies:
        copy.wait()


def back_kernel(
    nd, nz, gpp, part_ref, vec_ref, dw_ref, part_out, vec_out, dw_out, ssem, rsem, lsem
):
    d, z = lax.axis_index("dp"), lax.axis_index("tensor")
    t = lax.rem(d, 4)
    first = d - t
    everyone = []
    for kz in range(nz):
        for kd in range(nd):
            if kz or kd:
                everyone.append({"dp": lax.rem(d + kd, nd), "tensor": lax.rem(z + kz, nz)})
    greet(everyone)
    copies = []
    for k in range(1, 4):
        peer = lax.rem(t + k, 4)
        copies.append(
            remote(part_ref.at[peer], part_out.at[t], ssem.at[k], rsem.at[k], {"dp": first + peer})
        )
    for k in range(1, nd):
        copies.append(
            remote(vec_ref, vec_out.at[d], ssem.at[3 + k], rsem.at[3 + k], {"dp": lax.rem(d + k, nd)})
        )
    for copy in copies:
        copy.start()
    base = 3 + nd
    slot = z * gpp + d // 4

    def send_dw(k):
        dest = lax.rem(d + k, nd)
        return remote(
            dw_ref.at[dest],
            dw_out.at[slot],
            ssem.at[base + k],
            rsem.at[base + slot],
            {"dp": dest, "tensor": t},
        )

    own = pltpu.make_async_copy(dw_ref.at[d], dw_out.at[slot], lsem.at[0])
    for k in range(nd):
        if k == 0:

            @pl.when(t != z)
            def _():
                send_dw(0).start()

            @pl.when(t == z)
            def _():
                own.start()
        else:
            send_dw(k).start()
    part_out[t] = part_ref[t]
    vec_out[d] = vec_ref[...]
    for copy in copies:
        copy.wait()
    for k in range(nd):
        if k == 0:

            @pl.when(t != z)
            def _():
                send_dw(0).wait_send()

            @pl.when(t == z)
            def _():
                own.wait()
        else:
            send_dw(k).wait_send()
    for sz in range(nz):
        for k in range(gpp):
            source = 4 * k + z
            came = remote(
                dw_ref.at[0],
                dw_out.at[sz * gpp + k],
                ssem.at[base],
                rsem.at[base + sz * gpp + k],
                {"dp": source, "tensor": sz},
            )

            @pl.when(jnp.logical_or(source != d, z != sz))
            def _():
                came.wait_recv()


def combine_kernel(nd, nz, gpp, count, *refs):
    row_refs, (vec_ref,) = refs[:count], refs[count : count + 1]
    outs, (vec_out,) = refs[count + 1 : 2 * count + 1], refs[2 * count + 1 : 2 * count + 2]
    ssem, rsem, usend, urecv, dsend, drecv, vsend, vrecv, lsem = refs[2 * count + 2 :]
    d, z = lax.axis_index("dp"), lax.axis_index("tensor")
    t = lax.rem(d, 4)
    quarter = nd // 4
    plane = [{"dp": lax.rem(d + k, nd)} for k in range(1, nd)]
    column = [{"tensor": lax.rem(z + k, nz)} for k in range(1, nz)]
    greet(plane + column)
    vecs = []
    for k in range(1, nz):
        copy = remote(vec_ref, vec_out.at[z], vsend.at[k], vrecv.at[k], {"tensor": lax.rem(z + k, nz)})
        copy.start()
        vecs.append(copy)
    vec_out[z] = vec_ref[...]
    for i in range(count):
        for b in range(quarter):
            dest = t * quarter + b
            copy = remote(
                row_refs[i].at[b],
                outs[i].at[z, d // 4],
                ssem.at[i, b],
                rsem.at[i, d // 4],
                {"dp": dest},
            )
            own = pltpu.make_async_copy(row_refs[i].at[b], outs[i].at[z, d // 4], lsem.at[i])

            @pl.when(dest != d)
            def _():
                copy.start()

            @pl.when(dest == d)
            def _():
                own.start()

    def hop(i, k, up):
        block = z - k if up else z + k
        block = jnp.clip(block, 0, nz - 1)
        peer = jnp.clip(z + 1 if up else z - 1, 0, nz - 1)
        sems = (usend, urecv) if up else (dsend, drecv)
        return remote(
            outs[i].at[block], outs[i].at[block], sems[0].at[i, k], sems[1].at[i, k], {"tensor": peer}
        )

    def sends(k, up):
        return (z - k >= 0) & (z + 1 < nz) if up else (z + k < nz) & (z - 1 >= 0)

    def gets(k, up):
        return z - 1 - k >= 0 if up else z + 1 + k < nz

    def came(i, k, up):
        block = jnp.clip(z - 1 - k if up else z + 1 + k, 0, nz - 1)
        peer = jnp.clip(z - 1 if up else z + 1, 0, nz - 1)
        sems = (usend, urecv) if up else (dsend, drecv)
        return remote(
            outs[i].at[block], outs[i].at[block], sems[0].at[i, k], sems[1].at[i, k], {"tensor": peer}
        )

    for i in range(count):
        for k in range(gpp):
            source = 4 * k + d // quarter
            arrive = remote(
                row_refs[i].at[0], outs[i].at[z, k], ssem.at[i, 0], rsem.at[i, k], {"dp": source}
            )

            @pl.when(source != d)
            def _():
                arrive.wait_recv()

            @pl.when(source == d)
            def _():
                pltpu.make_async_copy(row_refs[i].at[0], outs[i].at[z, k], lsem.at[i]).wait()

        for up in (True, False):

            @pl.when(sends(0, up))
            def _():
                hop(i, 0, up).start()

    for k in range(nz - 1):
        for i in range(count):
            for up in (True, False):

                @pl.when(gets(k, up))
                def _():
                    came(i, k, up).wait_recv()

                if k + 1 < nz - 1:

                    @pl.when(sends(k + 1, up))
                    def _():
                        hop(i, k + 1, up).start()

    for k in range(nz - 1):
        for i in range(count):
            for up in (True, False):

                @pl.when(sends(k, up))
                def _():
                    hop(i, k, up).wait_send()

    for i in range(count):
        for b in range(quarter):
            dest = t * quarter + b
            copy = remote(
                row_refs[i].at[b],
                outs[i].at[z, d // 4],
                ssem.at[i, b],
                rsem.at[i, d // 4],
                {"dp": dest},
            )

            @pl.when(dest != d)
            def _():
                copy.wait_send()

    for copy in vecs:
        copy.wait()


def attend_kernel(heads, q_ref, kv_ref, segc_ref, segr_ref, mix_ref, lse_ref):
    width = heads * HEAD_DIM
    same = segc_ref[...] == segr_ref[...]
    lane = lax.broadcasted_iota(jnp.int32, lse_ref.shape, 1)
    lse_all = jnp.zeros(lse_ref.shape, F32)
    mixes = []
    for h in range(heads):
        cut = slice(h * HEAD_DIM, (h + 1) * HEAD_DIM)
        query = q_ref[:, cut]
        keys = kv_ref[:, width + h * HEAD_DIM : width + (h + 1) * HEAD_DIM]
        values = kv_ref[:, 2 * width + h * HEAD_DIM : 2 * width + (h + 1) * HEAD_DIM]
        scores = lax.dot_general(query, keys, (((1,), (1,)), ((), ())), preferred_element_type=F32)
        scores = jnp.where(same, scores, NEGATIVE)
        top = jnp.max(scores, axis=1, keepdims=True)
        powers = jnp.exp(scores - top)
        total = jnp.sum(powers, axis=1, keepdims=True)
        prob_low = (powers * (1.0 / total)).astype(BF16)
        mixes.append(jnp.dot(prob_low, values, preferred_element_type=F32).astype(BF16))
        lse_all = jnp.where(lane == h, top + jnp.log(total), lse_all)
    mix_ref[...] = jnp.concatenate(mixes, axis=1)
    lse_ref[...] = lse_all


def attend(qkv, seg_col, seg_row, heads, block):
    rows = qkv.shape[0]
    return pl.pallas_call(
        functools.partial(attend_kernel, heads),
        grid=(rows // block,),
        in_specs=[
            pl.BlockSpec((block, qkv.shape[1]), lambda i: (i, 0)),
            pl.BlockSpec((rows, qkv.shape[1]), lambda i: (0, 0)),
            pl.BlockSpec((block, 1), lambda i: (i, 0)),
            pl.BlockSpec((1, rows), lambda i: (0, 0)),
        ],
        out_specs=[
            pl.BlockSpec((block, heads * HEAD_DIM), lambda i: (i, 0)),
            pl.BlockSpec((block, 128), lambda i: (i, 0)),
        ],
        out_shape=[
            jax.ShapeDtypeStruct((rows, heads * HEAD_DIM), BF16),
            jax.ShapeDtypeStruct((rows, 128), F32),
        ],
        compiler_params=pltpu.CompilerParams(vmem_limit_bytes=VMEM_LIMIT),
    )(qkv, qkv, seg_col, seg_row)


def attend_back_kernel(
    heads, steps, q_ref, kv_ref, g_ref, lse_ref, segc_ref, segr_ref, dq_ref, dkv_ref, dk_acc, dv_acc
):
    step = pl.program_id(0)
    width = heads * HEAD_DIM
    same = segc_ref[...] == segr_ref[...]
    dqs = []
    for h in range(heads):
        cut = slice(h * HEAD_DIM, (h + 1) * HEAD_DIM)
        query = q_ref[:, cut]
        keys = kv_ref[:, width + h * HEAD_DIM : width + (h + 1) * HEAD_DIM]
        values = kv_ref[:, 2 * width + h * HEAD_DIM : 2 * width + (h + 1) * HEAD_DIM]
        grad = g_ref[:, cut]
        scores = lax.dot_general(query, keys, (((1,), (1,)), ((), ())), preferred_element_type=F32)
        scores = jnp.where(same, scores, NEGATIVE)
        probs = jnp.exp(scores - lse_ref[:, h : h + 1])
        grad_probs = lax.dot_general(
            grad, values, (((1,), (1,)), ((), ())), preferred_element_type=F32
        )
        inner = jnp.sum(grad_probs * probs, axis=1, keepdims=True)
        grad_scores = (probs * (grad_probs - inner)).astype(BF16)
        prob_low = probs.astype(BF16)
        dqs.append(jnp.dot(grad_scores, keys, preferred_element_type=F32))
        dk = lax.dot_general(
            grad_scores, query, (((0,), (0,)), ((), ())), preferred_element_type=F32
        )
        dv = lax.dot_general(prob_low, grad, (((0,), (0,)), ((), ())), preferred_element_type=F32)

        @pl.when(step == 0)
        def _():
            dk_acc[h] = dk
            dv_acc[h] = dv

        @pl.when(step > 0)
        def _():
            dk_acc[h] += dk
            dv_acc[h] += dv

    dq_ref[...] = (jnp.concatenate(dqs, axis=1).astype(BF16) * 0.125).astype(BF16)

    @pl.when(step == steps - 1)
    def _():
        dkv_ref[:, :width] = jnp.concatenate([dk_acc[h] for h in range(heads)], axis=1).astype(BF16)
        dkv_ref[:, width:] = jnp.concatenate([dv_acc[h] for h in range(heads)], axis=1).astype(BF16)


def attend_back(qkv, grad, lse, seg_col, seg_row, heads, block):
    rows = qkv.shape[0]
    width = heads * HEAD_DIM
    steps = rows // block
    return pl.pallas_call(
        functools.partial(attend_back_kernel, heads, steps),
        grid=(steps,),
        in_specs=[
            pl.BlockSpec((block, qkv.shape[1]), lambda i: (i, 0)),
            pl.BlockSpec((rows, qkv.shape[1]), lambda i: (0, 0)),
            pl.BlockSpec((block, width), lambda i: (i, 0)),
            pl.BlockSpec((block, 128), lambda i: (i, 0)),
            pl.BlockSpec((block, 1), lambda i: (i, 0)),
            pl.BlockSpec((1, rows), lambda i: (0, 0)),
        ],
        out_specs=[
            pl.BlockSpec((block, width), lambda i: (i, 0)),
            pl.BlockSpec((rows, 2 * width), lambda i: (0, 0)),
        ],
        out_shape=[
            jax.ShapeDtypeStruct((rows, width), BF16),
            jax.ShapeDtypeStruct((rows, 2 * width), BF16),
        ],
        scratch_shapes=[
            pltpu.VMEM((heads, rows, HEAD_DIM), F32),
            pltpu.VMEM((heads, rows, HEAD_DIM), F32),
        ],
        compiler_params=pltpu.CompilerParams(vmem_limit_bytes=VMEM_LIMIT),
    )(qkv, qkv, grad, lse, seg_col, seg_row)


def restore_kernel(count, loc_ref, *refs):
    ins, outs = refs[:count], refs[count:]
    block = outs[0].shape[0]
    row = lax.broadcasted_iota(jnp.int32, (block, loc_ref.shape[1]), 0) + pl.program_id(0) * block
    pick = jnp.where(row == loc_ref[...], 1.0, 0.0).astype(BF16)
    for i in range(count):
        outs[i][...] = jnp.dot(pick, ins[i][...], preferred_element_type=F32).astype(BF16)


def restore(loc_row, arrays, block):
    rows, width = arrays[0].shape
    count = len(arrays)
    return pl.pallas_call(
        functools.partial(restore_kernel, count),
        grid=(rows // block,),
        in_specs=[pl.BlockSpec((1, rows), lambda i: (0, 0))]
        + [pl.BlockSpec((rows, width), lambda i: (0, 0))] * count,
        out_specs=[pl.BlockSpec((block, width), lambda i: (i, 0))] * count,
        out_shape=[jax.ShapeDtypeStruct((rows, width), BF16)] * count,
        compiler_params=pltpu.CompilerParams(vmem_limit_bytes=VMEM_LIMIT),
    )(loc_row, *arrays)


def shards(
    tokens,
    cotangent,
    dealing,
    segments,
    w_query,
    w_key,
    w_value,
    b_query,
    b_value,
    w_out,
    b_out,
    gain_one,
    shift_one,
    w_up,
    b_up,
    w_down,
    b_down,
    gain_two,
    shift_two,
):
    nd, nz = lax.axis_size("dp"), lax.axis_size("tensor")
    rows, width = tokens.shape
    gpp = nd // 4
    per = rows // nd
    part = rows // 4
    slab = w_query.shape[0]
    cols = w_query.shape[1]
    heads = cols // HEAD_DIM
    ff = w_up.shape[1]
    d, z = lax.axis_index("dp"), lax.axis_index("tensor")
    t = d % 4
    sds = jax.ShapeDtypeStruct
    dma = pltpu.SemaphoreType.DMA

    shard = jnp.concatenate([w_up, w_down.T, w_out.T], axis=1).astype(BF16)
    whole = lax.all_gather(shard, ("tensor", "dp"), axis=0, tiled=True)
    whole = whole.reshape(nz, width, 2 * ff + cols)
    up_w, down_t, out_t = whole[:, :, :ff], whole[:, :, ff : 2 * ff], whole[:, :, 2 * ff :]

    pad = 16 - rows // 128
    meta = jnp.concatenate(
        [
            jnp.pad(dealing.reshape(rows // 128, 128), ((0, pad), (0, 0)), constant_values=-1),
            jnp.pad(segments.reshape(rows // 128, 128), ((0, pad), (0, 0))),
        ]
    )
    bias = jnp.concatenate([b_query, b_value, b_up]).reshape(-1, 128)
    bias_rows = bias.shape[0]
    bias = jnp.pad(bias, ((0, -bias_rows % 8), (0, 0)))
    n_meta = nd - 1 + nz - 1
    meta_all, bias_all = comm_call(
        functools.partial(meta_kernel, nd, nz),
        [sds((nd, 32, 128), jnp.int32), sds((nz,) + bias.shape, F32)],
        [dma((n_meta,)), dma((n_meta,))],
        0,
        (meta, bias),
    )
    bias_all = bias_all[:, :bias_rows].reshape(nz, bias_rows * 128)
    own_bias = lax.dynamic_index_in_dim(bias_all, t, 0, keepdims=False)
    bq, bv = own_bias[:cols], own_bias[cols : 2 * cols]
    bu = bias_all[:, 2 * cols :]

    loc_all, seg_in = pl.pallas_call(
        functools.partial(index_kernel, nd, gpp, rows),
        in_specs=[vmem_spec()],
        out_specs=[vmem_spec()] * 2,
        out_shape=[sds((nd, per, 1), jnp.int32), sds((nd, per, 1), jnp.int32)],
        compiler_params=pltpu.CompilerParams(vmem_limit_bytes=VMEM_LIMIT),
    )(meta_all)
    send_tok, send_cot = pl.pallas_call(
        functools.partial(gather_kernel, nd, gpp, rows),
        in_specs=[vmem_spec()] * 3,
        out_specs=[vmem_spec()] * 2,
        out_shape=[sds((gpp, per, width), BF16)] * 2,
        compiler_params=pltpu.CompilerParams(vmem_limit_bytes=VMEM_LIMIT),
    )(loc_all, tokens, cotangent)
    wqkv_shard = jnp.concatenate([w_query, w_key, w_value], axis=1).astype(BF16)
    n_disp = nd + max(nd, gpp * nz) + max(gpp, nd // 4)
    x_in, cot_in, wqkv = comm_call(
        functools.partial(dispatch_kernel, nd, nz, gpp),
        [sds((nd, per, width), BF16), sds((nd // 4, per, width), BF16), sds((nd, slab, 3 * cols), BF16)],
        [dma((n_disp,)), dma((n_disp,)), dma((3,))],
        1,
        (send_tok, send_cot, wqkv_shard),
    )
    x_in = x_in.reshape(rows, width)
    wqkv = wqkv.reshape(width, 3 * cols)
    seg_col = seg_in.reshape(rows, 1)
    seg_row = seg_in.reshape(1, rows)

    qkv = jnp.dot(x_in, wqkv, preferred_element_type=F32)
    scale = jnp.where(jnp.arange(3 * cols) < cols, 0.125, 1.0)
    qkv = ((qkv + jnp.concatenate([bq, jnp.zeros_like(bq), bv])) * scale).astype(BF16)
    mixed, lse = attend(qkv, seg_col, seg_row, heads, 256)

    quad = [dma((3,)), dma((3,))]
    (mixed_in,) = comm_call(
        functools.partial(quad_kernel, nd),
        [sds((4, part, cols), BF16)],
        quad,
        2,
        (mixed.reshape(4, part, cols),),
    )
    residual = lax.dynamic_slice_in_dim(x_in, t * part, part, 0).astype(F32)
    grad_out = cot_in.reshape(part, width).astype(F32)

    attn = jnp.einsum("tri,tdi->rd", mixed_in, out_t, preferred_element_type=F32)
    first_in = residual + attn + b_out
    first_norm = layer_norm(first_in, gain_one, shift_one)
    first_low = first_norm.astype(BF16)
    pre_act = jnp.einsum("rd,zdf->zrf", first_low, up_w, preferred_element_type=F32) + bu[:, None, :]
    hidden_low = exact_gelu(pre_act).astype(BF16)
    mlp = jnp.einsum("zrf,zdf->rd", hidden_low, down_t, preferred_element_type=F32)
    second_in = first_norm + mlp + b_down
    result = layer_norm(second_in, gain_two, shift_two)
    grad_second, gain2_grad, shift2_grad = norm_back(second_in, gain_two, shift_two, grad_out)
    branch_low = grad_second.astype(BF16)
    dbias_grad = jnp.sum(branch_low, axis=0, dtype=F32)
    down_grad = jnp.einsum("rd,zrf->zdf", branch_low, hidden_low, preferred_element_type=F32)
    grad_hidden = jnp.einsum("rd,zdf->zrf", branch_low, down_t, preferred_element_type=F32)
    grad_pre = jax.vjp(exact_gelu, pre_act)[1](grad_hidden)[0].astype(BF16)
    ubias_grad = jnp.sum(grad_pre, axis=1, dtype=F32)
    up_grad = jnp.einsum("rd,zrf->zdf", first_low, grad_pre, preferred_element_type=F32)
    back = jnp.einsum("zrf,zdf->rd", grad_pre, up_w, preferred_element_type=F32)
    grad_first = grad_second + back
    grad_attn_in, gain1_grad, shift1_grad = norm_back(first_in, gain_one, shift_one, grad_first)
    attn_low = grad_attn_in.astype(BF16)
    obias_grad = jnp.sum(attn_low, axis=0, dtype=F32)
    out_grad = jnp.einsum("rd,tri->tdi", attn_low, mixed_in, preferred_element_type=F32)
    grad_mixed = jnp.einsum("rd,tdi->tri", attn_low, out_t, preferred_element_type=F32).astype(BF16)

    w_grads = jnp.concatenate([up_grad, down_grad, out_grad], axis=2).astype(BF16)
    w_grads = lax.psum_scatter(
        w_grads.reshape(nz * width, 2 * ff + cols), ("tensor", "dp"), scatter_dimension=0, tiled=True
    ).astype(F32)

    (grad_in_mixed,) = comm_call(
        functools.partial(quad_kernel, nd), [sds((4, part, cols), BF16)], quad, 3, (grad_mixed,)
    )
    grad_in_mixed = grad_in_mixed.reshape(rows, cols)
    dq, dkv = attend_back(qkv, grad_in_mixed, lse, seg_col, seg_row, heads, 256)
    dqkv = jnp.concatenate([dq, dkv], axis=1)
    bias_sums = jnp.sum(dqkv, axis=0, dtype=F32)
    back_part = jnp.einsum("rc,dc->rd", dqkv, wqkv, preferred_element_type=F32).astype(BF16)
    dw = jnp.einsum("rd,rc->dc", x_in, dqkv, preferred_element_type=F32).astype(BF16)
    mine = (jnp.arange(nz) == t)[:, None]
    vec = jnp.concatenate(
        [
            jnp.where(mine, bias_sums[:cols], 0.0).reshape(-1),
            jnp.where(mine, bias_sums[2 * cols :], 0.0).reshape(-1),
            obias_grad,
            gain1_grad,
            shift1_grad,
            dbias_grad,
            gain2_grad,
            shift2_grad,
            ubias_grad.reshape(-1),
        ]
    ).reshape(-1, 128)
    n_back = 3 + nd + max(nd, nz * gpp)
    part_in, vec_in, dw_in = comm_call(
        functools.partial(back_kernel, nd, nz, gpp),
        [sds((4, part, width), BF16), sds((nd,) + vec.shape, F32), sds((nz * gpp, slab, 3 * cols), BF16)],
        [dma((n_back,)), dma((n_back,)), dma((1,))],
        4,
        (back_part.reshape(4, part, width), vec, dw.reshape(nd, slab, 3 * cols)),
    )
    grad_in = grad_attn_in + jnp.sum(part_in, axis=0, dtype=F32)
    dw_sum = jnp.sum(dw_in, axis=0, dtype=F32)
    vec_plane = jnp.sum(vec_in, axis=0)
    quarter = nd // 4
    block = (quarter, per, width)
    got, got_grad, vec_z = comm_call(
        functools.partial(combine_kernel, nd, nz, gpp, 2),
        [sds((nz, gpp, per, width), BF16)] * 2 + [sds((nz,) + vec.shape, F32)],
        [
            dma((2, quarter)),
            dma((2, gpp)),
            dma((2, nz)),
            dma((2, nz)),
            dma((2, nz)),
            dma((2, nz)),
            dma((nz,)),
            dma((nz,)),
            dma((2,)),
        ],
        5,
        (result.astype(BF16).reshape(block), grad_in.astype(BF16).reshape(block), vec_plane),
    )
    layer_out, grad_tokens = restore(
        loc_all.reshape(1, rows), (got.reshape(rows, width), got_grad.reshape(rows, width)), 256
    )
    vec_all = jnp.sum(vec_z, axis=0).reshape(-1)
    q_all, v_all = vec_all[:width].reshape(nz, cols), vec_all[width : 2 * width].reshape(nz, cols)
    rest = vec_all[2 * width : 8 * width].reshape(6, width)
    u_all = vec_all[8 * width :].reshape(nz, ff)

    def mine_of(array):
        return lax.dynamic_index_in_dim(array, z, 0, keepdims=False)

    return (
        layer_out,
        grad_tokens,
        dw_sum[:, :cols],
        dw_sum[:, cols : 2 * cols],
        dw_sum[:, 2 * cols :],
        mine_of(q_all),
        mine_of(v_all),
        w_grads[:, 2 * ff :].T,
        rest[0],
        rest[1],
        rest[2],
        w_grads[:, :ff],
        mine_of(u_all),
        w_grads[:, ff : 2 * ff].T,
        rest[3],
        rest[4],
        rest[5],
    )


def solution(mesh):
    in_specs = (
        P("dp", None),
        P("dp", None),
        P("dp"),
        P("dp", None),
        P("dp", "tensor"),
        P("dp", "tensor"),
        P("dp", "tensor"),
        P("tensor"),
        P("tensor"),
        P("tensor", "dp"),
        P(),
        P(),
        P(),
        P("dp", "tensor"),
        P("tensor"),
        P("tensor", "dp"),
        P(),
        P(),
        P(),
    )
    out_specs = (
        P("dp", None),
        P("dp", None),
        P("dp", "tensor"),
        P("dp", "tensor"),
        P("dp", "tensor"),
        P("tensor"),
        P("tensor"),
        P("tensor", "dp"),
        P(),
        P(),
        P(),
        P("dp", "tensor"),
        P("tensor"),
        P("tensor", "dp"),
        P(),
        P(),
        P(),
    )
    return jax.shard_map(shards, mesh=mesh, in_specs=in_specs, out_specs=out_specs, check_vma=False)
```

```python
import functools

import jax
import jax.numpy as jnp
from jax import lax
from jax.experimental import pallas as pl
from jax.experimental.pallas import tpu as pltpu
from jax.sharding import PartitionSpec as P

HEAD_DIM = 64
EPSILON = 1e-05
NEGATIVE = -1e30
MESH = pl.DeviceIdType.MESH
F32 = jnp.float32
BF16 = jnp.bfloat16
DP = ("pair", "core")
VMEM_LIMIT = 56 * 1024 * 1024


def place():
    return lax.axis_index("pair") * 2 + lax.axis_index("core"), lax.axis_index("tensor")


def at(dp, tensor=None):
    device = {"pair": dp // 2, "core": lax.rem(dp, 2)}
    return device if tensor is None else {**device, "tensor": tensor}


def vmem_spec():
    return pl.BlockSpec(memory_space=pltpu.VMEM)


def remote(src, dst, send_sem, recv_sem, device):
    return pltpu.make_async_remote_copy(
        src_ref=src,
        dst_ref=dst,
        send_sem=send_sem,
        recv_sem=recv_sem,
        device_id=device,
        device_id_type=MESH,
    )


def greet(devices):
    barrier = pltpu.get_barrier_semaphore()
    for device in devices:
        pl.semaphore_signal(barrier, inc=1, device_id=device, device_id_type=MESH)
    pl.semaphore_wait(barrier, len(devices))


def comm_call(kernel, out_shape, scratch, cid, args, in_place=0):
    def specs(count):
        return [vmem_spec()] * (count - in_place) + [pl.BlockSpec(memory_space=pl.ANY)] * in_place

    return pl.pallas_call(
        kernel,
        out_shape=out_shape,
        in_specs=specs(len(args)),
        out_specs=specs(len(out_shape)),
        scratch_shapes=scratch,
        compiler_params=pltpu.CompilerParams(
            collective_id=cid, has_side_effects=True, vmem_limit_bytes=VMEM_LIMIT
        ),
    )(*args)


def meta_kernel(nd, nz, meta_ref, bias_ref, meta_out, bias_out, ssem, rsem):
    d, z = place()
    plane = [at(lax.rem(d + k, nd)) for k in range(1, nd)]
    column = [{"tensor": lax.rem(z + k, nz)} for k in range(1, nz)]
    greet(plane + column)
    copies = []
    for i, device in enumerate(plane):
        copies.append(remote(meta_ref, meta_out.at[d], ssem.at[i], rsem.at[i], device))
    for j, device in enumerate(column):
        i = len(plane) + j
        copies.append(remote(bias_ref, bias_out.at[z], ssem.at[i], rsem.at[i], device))
    for copy in copies:
        copy.start()
    meta_out[d] = meta_ref[...]
    bias_out[z] = bias_ref[...]
    for copy in copies:
        copy.wait()


def index_kernel(nd, gpp, rows, meta_ref, loc_ref, seg_ref):
    per = rows // nd
    d, z = place()
    group = z * gpp + d // 4
    lane_i = lax.broadcasted_iota(jnp.int32, (128, 128), 0)
    lane_j = lax.broadcasted_iota(jnp.int32, (128, 128), 1)
    upper = (lane_i <= lane_j).astype(F32)
    row_i = lax.broadcasted_iota(jnp.int32, (16, 16), 0)
    row_j = lax.broadcasted_iota(jnp.int32, (16, 16), 1)
    lower = (row_j < row_i).astype(F32)
    rank_of = lax.broadcasted_iota(jnp.int32, (per, 128), 0).astype(F32)

    def pick(deal, source, values):
        low = source * rows
        hit = (deal >= low) & (deal < low + rows)
        ones = jnp.where(hit, 1.0, 0.0)
        inner = jnp.dot(ones, upper, preferred_element_type=F32)
        total = jnp.broadcast_to(inner[:, 127:128], (16, 128))
        before = jnp.dot(lower, total, preferred_element_type=F32)
        key = jnp.where(hit, inner + before - 1.0, -1.0)
        found = jnp.zeros((per, 128), F32)
        for c in range(rows // 128):
            found = found + jnp.where(rank_of == key[c : c + 1, :], values[c : c + 1, :], 0.0)
        return jnp.sum(found, axis=1, keepdims=True).astype(jnp.int32)

    for g in range(nd):
        deal = meta_ref[g, 0:16, :]
        loc_ref[g] = pick(deal, d, (deal - d * rows).astype(F32))
    own_deal = meta_ref[group, 0:16, :]
    own_seg = meta_ref[group, 16:32, :].astype(F32)
    for s in range(nd):
        seg_ref[s] = pick(own_deal, s, own_seg)


def gather_kernel(nd, gpp, rows, loc_ref, tok_ref, cot_ref, tok_out, cot_out):
    per = rows // nd
    _, z = place()
    column = lax.broadcasted_iota(jnp.int32, (per, rows), 1)
    for k in range(gpp):
        loc = loc_ref[z * gpp + k]
        pick = jnp.where(column == loc, 1.0, 0.0).astype(BF16)
        tok_out[k] = jnp.dot(pick, tok_ref[...], preferred_element_type=F32).astype(BF16)
        cot_out[k] = jnp.dot(pick, cot_ref[...], preferred_element_type=F32).astype(BF16)


def dispatch_kernel(
    nd, nz, gpp, tok_ref, cot_ref, wqkv_ref, x_out, cot_out, w_out, ssem, rsem, lsem
):
    d, z = place()
    t = lax.rem(d, 4)
    quarter = nd // 4
    everyone = []
    for kz in range(nz):
        for kd in range(nd):
            if kz or kd:
                everyone.append(at(lax.rem(d + kd, nd), lax.rem(z + kz, nz)))
    greet(everyone)
    waits = []
    locals_ = []
    for k in range(1, nd):
        dest = lax.rem(d + k, nd)
        copy = remote(tok_ref.at[dest // 4], x_out.at[d], ssem.at[k], rsem.at[k], at(dest))
        copy.start()
        waits.append(copy)
    own = pltpu.make_async_copy(tok_ref.at[d // 4], x_out.at[d], lsem.at[0])
    own.start()
    locals_.append(own)
    base = nd
    for m in range(gpp):
        for kz in range(nz):
            dest = 4 * m + z
            dz = lax.rem(z + kz, nz)
            copy = remote(
                wqkv_ref,
                w_out.at[d],
                ssem.at[base + m * nz + kz],
                rsem.at[base + d],
                at(dest, dz),
            )
            if kz == 0:

                @pl.when(dest != d)
                def _():
                    copy.start()

                @pl.when(dest == d)
                def _():
                    pltpu.make_async_copy(wqkv_ref, w_out.at[d], lsem.at[1]).start()
            else:
                copy.start()
    base_c = base + max(nd, gpp * nz)
    for k in range(gpp):
        dest = 4 * k + d // quarter
        copy = remote(
            cot_ref.at[k],
            cot_out.at[lax.rem(d, quarter)],
            ssem.at[base_c + k],
            rsem.at[base_c + lax.rem(d, quarter)],
            at(dest),
        )

        @pl.when(dest != d)
        def _():
            copy.start()

        @pl.when(dest == d)
        def _():
            pltpu.make_async_copy(
                cot_ref.at[k], cot_out.at[lax.rem(d, quarter)], lsem.at[2]
            ).start()

    for copy in waits:
        copy.wait()
    for copy in locals_:
        copy.wait()
    for m in range(gpp):
        for kz in range(nz):
            dest = 4 * m + z
            send = remote(
                wqkv_ref,
                w_out.at[d],
                ssem.at[base + m * nz + kz],
                rsem.at[base + d],
                at(dest, lax.rem(z + kz, nz)),
            )
            if kz == 0:

                @pl.when(dest != d)
                def _():
                    send.wait_send()

                @pl.when(dest == d)
                def _():
                    pltpu.make_async_copy(wqkv_ref, w_out.at[d], lsem.at[1]).wait()
            else:
                send.wait_send()
    for s in range(nd):
        came = remote(
            wqkv_ref, w_out.at[s], ssem.at[base], rsem.at[base + s], at(s, t)
        )

        @pl.when(jnp.logical_or(t != z, d != s))
        def _():
            came.wait_recv()

    for k in range(gpp):
        dest = 4 * k + d // quarter
        send = remote(
            cot_ref.at[k],
            cot_out.at[lax.rem(d, quarter)],
            ssem.at[base_c + k],
            rsem.at[base_c + lax.rem(d, quarter)],
            at(dest),
        )

        @pl.when(dest != d)
        def _():
            send.wait_send()

        @pl.when(dest == d)
        def _():
            pltpu.make_async_copy(
                cot_ref.at[k], cot_out.at[lax.rem(d, quarter)], lsem.at[2]
            ).wait()

    for j in range(quarter):
        source = t * quarter + j
        came = remote(
            cot_ref.at[0], cot_out.at[j], ssem.at[base_c], rsem.at[base_c + j], at(source)
        )

        @pl.when(source != d)
        def _():
            came.wait_recv()


def quad_kernel(in_ref, big_ref, out_ref, big_out, ssem, rsem):
    d, _ = place()
    t = lax.rem(d, 4)
    first = d - t
    peers = [lax.rem(t + k, 4) for k in range(1, 4)]
    greet([at(first + peer) for peer in peers])
    core = lax.rem(t, 2)
    copies = []
    for i, peer in enumerate(peers):
        copies.append(
            remote(in_ref.at[peer], out_ref.at[t], ssem.at[i], rsem.at[i], at(first + peer))
        )
    copies.append(remote(big_ref, big_out, ssem.at[3], rsem.at[3], at(d + 1 - 2 * core)))
    for copy in copies:
        copy.start()
    out_ref[t] = in_ref[t]
    for copy in copies:
        copy.wait()


def back_kernel(nd, gpp, part_ref, vec_ref, dw_ref, part_out, vec_out, dw_out, ssem, rsem):
    d, _ = place()
    t = lax.rem(d, 4)
    group = d // 4
    greet([at(lax.rem(d + k, nd)) for k in range(1, nd)])
    other = d - t + lax.rem(t + 2, 4)
    copies = [remote(part_ref.at[1 - t // 2], part_out, ssem.at[0], rsem.at[0], at(other))]
    for k in range(1, gpp):
        peer = lax.rem(group + k, gpp)
        copies.append(
            remote(dw_ref.at[peer], dw_out.at[group], ssem.at[k], rsem.at[k], at(4 * peer + t))
        )
    for k in range(1, nd):
        i = gpp + k
        copies.append(
            remote(vec_ref, vec_out.at[d], ssem.at[i], rsem.at[i], at(lax.rem(d + k, nd)))
        )
    for copy in copies:
        copy.start()
    dw_out[group] = dw_ref[group]
    vec_out[d] = vec_ref[...]
    for copy in copies:
        copy.wait()


def combine_kernel(nd, nz, gpp, count, *refs):
    row_refs, (vec_ref, dw_ref) = refs[:count], refs[count : count + 2]
    outs, (vec_out, dw_out) = refs[count + 2 : 2 * count + 2], refs[2 * count + 2 : 2 * count + 4]
    ssem, rsem, usend, urecv, dsend, drecv, vsend, vrecv, wsend, wrecv, lsem = refs[2 * count + 4 :]
    d, z = place()
    t = lax.rem(d, 4)
    quarter = nd // 4
    everyone = []
    for kz in range(nz):
        for kd in range(nd):
            if kz or kd:
                everyone.append(at(lax.rem(d + kd, nd), lax.rem(z + kz, nz)))
    greet(everyone)
    vecs = []
    for k in range(1, nz):
        copy = remote(vec_ref, vec_out.at[z], vsend.at[k], vrecv.at[k], {"tensor": lax.rem(z + k, nz)})
        copy.start()
        vecs.append(copy)
    vec_out[z] = vec_ref[...]
    for i in range(count):
        for b in range(quarter):
            dest = t * quarter + b
            copy = remote(
                row_refs[i].at[b],
                outs[i].at[z, d // 4],
                ssem.at[i, b],
                rsem.at[i, d // 4],
                at(dest),
            )
            own = pltpu.make_async_copy(row_refs[i].at[b], outs[i].at[z, d // 4], lsem.at[i])

            @pl.when(dest != d)
            def _():
                copy.start()

            @pl.when(dest == d)
            def _():
                own.start()

    own_dw = pltpu.make_async_copy(dw_ref.at[t], dw_out.at[z], lsem.at[count])

    def send_dw(j):
        return remote(
            dw_ref.at[j], dw_out.at[z], wsend.at[j], wrecv.at[z], at(d - t + j, t)
        )

    for j in range(4):
        mine = (j == t) & (t == z)

        @pl.when(jnp.logical_not(mine))
        def _():
            send_dw(j).start()

        @pl.when(mine)
        def _():
            own_dw.start()

    def hop(i, k, up):
        block = z - k if up else z + k
        block = jnp.clip(block, 0, nz - 1)
        peer = jnp.clip(z + 1 if up else z - 1, 0, nz - 1)
        sems = (usend, urecv) if up else (dsend, drecv)
        return remote(
            outs[i].at[block], outs[i].at[block], sems[0].at[i, k], sems[1].at[i, k], {"tensor": peer}
        )

    def sends(k, up):
        return (z - k >= 0) & (z + 1 < nz) if up else (z + k < nz) & (z - 1 >= 0)

    def gets(k, up):
        return z - 1 - k >= 0 if up else z + 1 + k < nz

    def came(i, k, up):
        block = jnp.clip(z - 1 - k if up else z + 1 + k, 0, nz - 1)
        peer = jnp.clip(z - 1 if up else z + 1, 0, nz - 1)
        sems = (usend, urecv) if up else (dsend, drecv)
        return remote(
            outs[i].at[block], outs[i].at[block], sems[0].at[i, k], sems[1].at[i, k], {"tensor": peer}
        )

    for i in range(count):
        for k in range(gpp):
            source = 4 * k + d // quarter
            arrive = remote(
                row_refs[i].at[0], outs[i].at[z, k], ssem.at[i, 0], rsem.at[i, k], at(source)
            )

            @pl.when(source != d)
            def _():
                arrive.wait_recv()

            @pl.when(source == d)
            def _():
                pltpu.make_async_copy(row_refs[i].at[0], outs[i].at[z, k], lsem.at[i]).wait()

        for up in (True, False):

            @pl.when(sends(0, up))
            def _():
                hop(i, 0, up).start()

    for k in range(nz - 1):
        for i in range(count):
            for up in (True, False):

                @pl.when(gets(k, up))
                def _():
                    came(i, k, up).wait_recv()

                if k + 1 < nz - 1:

                    @pl.when(sends(k + 1, up))
                    def _():
                        hop(i, k + 1, up).start()

    for k in range(nz - 1):
        for i in range(count):
            for up in (True, False):

                @pl.when(sends(k, up))
                def _():
                    hop(i, k, up).wait_send()

    for i in range(count):
        for b in range(quarter):
            dest = t * quarter + b
            copy = remote(
                row_refs[i].at[b],
                outs[i].at[z, d // 4],
                ssem.at[i, b],
                rsem.at[i, d // 4],
                at(dest),
            )

            @pl.when(dest != d)
            def _():
                copy.wait_send()

    for j in range(4):
        mine = (j == t) & (t == z)

        @pl.when(jnp.logical_not(mine))
        def _():
            send_dw(j).wait_send()

        @pl.when(mine)
        def _():
            own_dw.wait()

    for sz in range(nz):
        source = d - t + z
        came_dw = remote(
            dw_ref.at[0], dw_out.at[sz], wsend.at[0], wrecv.at[sz], at(source, sz)
        )

        @pl.when(jnp.logical_or(source != d, z != sz))
        def _():
            came_dw.wait_recv()

    for copy in vecs:
        copy.wait()


def attend_kernel(heads, q_ref, kv_ref, segc_ref, segr_ref, mix_ref, lse_ref):
    width = heads * HEAD_DIM
    same = segc_ref[...] == segr_ref[...]
    lane = lax.broadcasted_iota(jnp.int32, lse_ref.shape, 1)
    lse_all = jnp.zeros(lse_ref.shape, F32)
    mixes = []
    for h in range(heads):
        cut = slice(h * HEAD_DIM, (h + 1) * HEAD_DIM)
        query = q_ref[:, cut]
        keys = kv_ref[:, width + h * HEAD_DIM : width + (h + 1) * HEAD_DIM]
        values = kv_ref[:, 2 * width + h * HEAD_DIM : 2 * width + (h + 1) * HEAD_DIM]
        scores = lax.dot_general(query, keys, (((1,), (1,)), ((), ())), preferred_element_type=F32)
        scores = jnp.where(same, scores, NEGATIVE)
        top = jnp.max(scores, axis=1, keepdims=True)
        powers = jnp.exp(scores - top)
        total = jnp.sum(powers, axis=1, keepdims=True)
        prob_low = (powers * (1.0 / total)).astype(BF16)
        mixes.append(jnp.dot(prob_low, values, preferred_element_type=F32).astype(BF16))
        lse_all = jnp.where(lane == h, top + jnp.log(total), lse_all)
    mix_ref[...] = jnp.concatenate(mixes, axis=1)
    lse_ref[...] = lse_all


def attend(qkv, seg_col, seg_row, heads, block):
    rows = qkv.shape[0]
    return pl.pallas_call(
        functools.partial(attend_kernel, heads),
        grid=(rows // block,),
        in_specs=[
            pl.BlockSpec((block, qkv.shape[1]), lambda i: (i, 0)),
            pl.BlockSpec((rows, qkv.shape[1]), lambda i: (0, 0)),
            pl.BlockSpec((block, 1), lambda i: (i, 0)),
            pl.BlockSpec((1, rows), lambda i: (0, 0)),
        ],
        out_specs=[
            pl.BlockSpec((block, heads * HEAD_DIM), lambda i: (i, 0)),
            pl.BlockSpec((block, 128), lambda i: (i, 0)),
        ],
        out_shape=[
            jax.ShapeDtypeStruct((rows, heads * HEAD_DIM), BF16),
            jax.ShapeDtypeStruct((rows, 128), F32),
        ],
        compiler_params=pltpu.CompilerParams(vmem_limit_bytes=VMEM_LIMIT),
    )(qkv, qkv, seg_col, seg_row)


def attend_back_kernel(
    heads, steps, q_ref, kv_ref, g_ref, lse_ref, segc_ref, segr_ref, dq_ref, dkv_ref, dk_acc, dv_acc
):
    step = pl.program_id(0)
    width = heads * HEAD_DIM
    same = segc_ref[...] == segr_ref[...]
    dqs = []
    for h in range(heads):
        cut = slice(h * HEAD_DIM, (h + 1) * HEAD_DIM)
        query = q_ref[:, cut]
        keys = kv_ref[:, width + h * HEAD_DIM : width + (h + 1) * HEAD_DIM]
        values = kv_ref[:, 2 * width + h * HEAD_DIM : 2 * width + (h + 1) * HEAD_DIM]
        grad = g_ref[:, cut]
        scores = lax.dot_general(query, keys, (((1,), (1,)), ((), ())), preferred_element_type=F32)
        scores = jnp.where(same, scores, NEGATIVE)
        probs = jnp.exp(scores - lse_ref[:, h : h + 1])
        grad_probs = lax.dot_general(
            grad, values, (((1,), (1,)), ((), ())), preferred_element_type=F32
        )
        inner = jnp.sum(grad_probs * probs, axis=1, keepdims=True)
        grad_scores = (probs * (grad_probs - inner)).astype(BF16)
        prob_low = probs.astype(BF16)
        dqs.append(jnp.dot(grad_scores, keys, preferred_element_type=F32))
        dk = lax.dot_general(
            grad_scores, query, (((0,), (0,)), ((), ())), preferred_element_type=F32
        )
        dv = lax.dot_general(prob_low, grad, (((0,), (0,)), ((), ())), preferred_element_type=F32)

        @pl.when(step == 0)
        def _():
            dk_acc[h] = dk
            dv_acc[h] = dv

        @pl.when(step > 0)
        def _():
            dk_acc[h] += dk
            dv_acc[h] += dv

    dq_ref[...] = (jnp.concatenate(dqs, axis=1).astype(BF16) * 0.125).astype(BF16)

    @pl.when(step == steps - 1)
    def _():
        dkv_ref[:, :width] = jnp.concatenate([dk_acc[h] for h in range(heads)], axis=1).astype(BF16)
        dkv_ref[:, width:] = jnp.concatenate([dv_acc[h] for h in range(heads)], axis=1).astype(BF16)


def attend_back(qkv, grad, lse, seg_col, seg_row, heads, block):
    rows = qkv.shape[0]
    width = heads * HEAD_DIM
    steps = rows // block
    return pl.pallas_call(
        functools.partial(attend_back_kernel, heads, steps),
        grid=(steps,),
        in_specs=[
            pl.BlockSpec((block, qkv.shape[1]), lambda i: (i, 0)),
            pl.BlockSpec((rows, qkv.shape[1]), lambda i: (0, 0)),
            pl.BlockSpec((block, width), lambda i: (i, 0)),
            pl.BlockSpec((block, 128), lambda i: (i, 0)),
            pl.BlockSpec((block, 1), lambda i: (i, 0)),
            pl.BlockSpec((1, rows), lambda i: (0, 0)),
        ],
        out_specs=[
            pl.BlockSpec((block, width), lambda i: (i, 0)),
            pl.BlockSpec((rows, 2 * width), lambda i: (0, 0)),
        ],
        out_shape=[
            jax.ShapeDtypeStruct((rows, width), BF16),
            jax.ShapeDtypeStruct((rows, 2 * width), BF16),
        ],
        scratch_shapes=[
            pltpu.VMEM((heads, rows, HEAD_DIM), F32),
            pltpu.VMEM((heads, rows, HEAD_DIM), F32),
        ],
        compiler_params=pltpu.CompilerParams(vmem_limit_bytes=VMEM_LIMIT),
    )(qkv, qkv, grad, lse, seg_col, seg_row)


def norm_parts(rows_in):
    center = rows_in - jnp.mean(rows_in, axis=-1, keepdims=True)
    spread = jnp.mean(center * center, axis=-1, keepdims=True)
    scale = lax.rsqrt(spread + EPSILON)
    return center * scale, scale


def norm_grad(normed, scale, gain, upstream):
    e = upstream * gain
    mean_e = jnp.mean(e, axis=-1, keepdims=True)
    mean_en = jnp.mean(e * normed, axis=-1, keepdims=True)
    return scale * (e - mean_e - normed * mean_en)


def dot_nt(left, right):
    return lax.dot_general(left, right, (((1,), (1,)), ((), ())), preferred_element_type=F32)


def dot_nn(left, right):
    return jnp.dot(left, right, preferred_element_type=F32)


def rowwise_kernel(
    nz,
    half,
    x_ref,
    mix_ref,
    cot_ref,
    own_ref,
    oth_ref,
    bu_ref,
    par_ref,
    res_ref,
    gin_ref,
    gmix_ref,
    down_ref,
    doth_ref,
    ub_ref,
    vec_ref,
    slope_s,
    hid_s,
    acc_s,
    first_s,
    first_t,
    branch_t,
    norm_s,
):
    core = lax.axis_index("core")
    halves = ((own_ref, down_ref), (oth_ref, doth_ref))
    out0, out1 = 2 * half, 2 * half + mix_ref.shape[2] // 2
    mid = mix_ref.shape[2] // 2
    b_out, gain1, shift1 = par_ref[0:1, :], par_ref[1:2, :], par_ref[2:3, :]
    b_down, gain2, shift2 = par_ref[3:4, :], par_ref[4:5, :], par_ref[5:6, :]

    def mix_halves(q):
        low, high = mix_ref[q, :, 0:mid], mix_ref[q, :, mid : 2 * mid]
        return jnp.where(core == 0, low, high), jnp.where(core == 0, high, low)

    total = x_ref[...].astype(F32) + b_out
    for q in range(nz):
        for part, (weights, _) in zip(mix_halves(q), halves):
            total = total + dot_nt(part, weights[q, :, out0:out1])
    normed1, scale1 = norm_parts(total)
    norm_s[...] = normed1
    first_norm = normed1 * gain1 + shift1
    first_low = first_norm.astype(BF16)
    first_s[...] = first_low
    first_t[...] = first_norm.T.astype(BF16)
    acc_s[...] = first_norm + b_down

    def forward(q, carry):
        for h, (weights, _) in enumerate(halves):
            pre = dot_nn(first_s[...], weights[q, :, 0:half]) + bu_ref[q, h : h + 1, :]
            phi_cum = 0.5 + 0.5 * lax.erf(pre * (0.5**0.5))
            density = jnp.exp(-0.5 * pre * pre) * 0.3989422804014327
            hidden = (pre * phi_cum).astype(BF16)
            slope_s[q, h] = phi_cum + pre * density
            hid_s[q, h] = hidden
            acc_s[...] += dot_nt(hidden, weights[q, :, half : 2 * half])
        return carry

    lax.fori_loop(0, nz, forward, 0)
    normed2, scale2 = norm_parts(acc_s[...])
    res_ref[...] = (normed2 * gain2 + shift2).astype(BF16)
    upstream = cot_ref[...].astype(F32)
    vec_ref[4:5, :] = jnp.sum(upstream * normed2, axis=0, keepdims=True)
    vec_ref[5:6, :] = jnp.sum(upstream, axis=0, keepdims=True)
    grad_second = norm_grad(normed2, scale2, gain2, upstream)
    branch_low = grad_second.astype(BF16)
    vec_ref[3:4, :] = jnp.sum(branch_low.astype(F32), axis=0, keepdims=True)
    branch_t[...] = grad_second.T.astype(BF16)
    res_b = branch_low
    acc_s[...] = grad_second

    def backward(q, carry):
        for h, (weights, grads) in enumerate(halves):
            grad_hidden = dot_nn(res_b, weights[q, :, half : 2 * half])
            grad_pre = (grad_hidden * slope_s[q, h]).astype(BF16)
            ub_ref[q, h : h + 1, :] = jnp.sum(grad_pre.astype(F32), axis=0, keepdims=True)
            acc_s[...] += dot_nt(grad_pre, weights[q, :, 0:half])
            grads[q, :, 0:half] = dot_nn(first_t[...], grad_pre).astype(BF16)
            grads[q, :, half : 2 * half] = dot_nn(branch_t[...], hid_s[q, h]).astype(BF16)
        return carry

    lax.fori_loop(0, nz, backward, 0)
    grad_first = acc_s[...]
    vec_ref[1:2, :] = jnp.sum(grad_first * norm_s[...], axis=0, keepdims=True)
    vec_ref[2:3, :] = jnp.sum(grad_first, axis=0, keepdims=True)
    grad_in = norm_grad(norm_s[...], scale1, gain1, grad_first)
    gin_ref[...] = grad_in
    attn_low = grad_in.astype(BF16)
    vec_ref[0:1, :] = jnp.sum(attn_low.astype(F32), axis=0, keepdims=True)
    vec_ref[6:8, :] = jnp.zeros((2, vec_ref.shape[1]), F32)
    attn_t = grad_in.T.astype(BF16)
    for q in range(nz):
        back = []
        for part, (weights, grads) in zip(mix_halves(q), halves):
            grads[q, :, out0:out1] = dot_nn(attn_t, part).astype(BF16)
            back.append(dot_nn(attn_low, weights[q, :, out0:out1]).astype(BF16))
        low = jnp.where(core == 0, back[0], back[1])
        high = jnp.where(core == 0, back[1], back[0])
        gmix_ref[q] = jnp.concatenate([low, high], axis=1)


def rowwise(x, mixed, cot, own, oth, bu, params):
    rows, width = x.shape
    nz, cols = mixed.shape[0], mixed.shape[2]
    half = bu.shape[2]
    sds = jax.ShapeDtypeStruct
    return pl.pallas_call(
        functools.partial(rowwise_kernel, nz, half),
        in_specs=[vmem_spec()] * 7,
        out_specs=[vmem_spec()] * 7,
        out_shape=[
            sds((rows, width), BF16),
            sds((rows, width), F32),
            sds((nz, rows, cols), BF16),
            sds(own.shape, BF16),
            sds(own.shape, BF16),
            sds((nz, 2, half), F32),
            sds((8, width), F32),
        ],
        scratch_shapes=[
            pltpu.VMEM((nz, 2, rows, half), F32),
            pltpu.VMEM((nz, 2, rows, half), BF16),
            pltpu.VMEM((rows, width), F32),
            pltpu.VMEM((rows, width), BF16),
            pltpu.VMEM((width, rows), BF16),
            pltpu.VMEM((width, rows), BF16),
            pltpu.VMEM((rows, width), F32),
        ],
        compiler_params=pltpu.CompilerParams(vmem_limit_bytes=VMEM_LIMIT),
    )(x, mixed, cot, own, oth, bu, params)


def restore_kernel(count, loc_ref, *refs):
    ins, outs = refs[:count], refs[count:]
    block = outs[0].shape[0]
    row = lax.broadcasted_iota(jnp.int32, (block, loc_ref.shape[1]), 0) + pl.program_id(0) * block
    pick = jnp.where(row == loc_ref[...], 1.0, 0.0).astype(BF16)
    for i in range(count):
        outs[i][...] = jnp.dot(pick, ins[i][...], preferred_element_type=F32).astype(BF16)


def restore(loc_row, arrays, block):
    rows, width = arrays[0].shape
    count = len(arrays)
    return pl.pallas_call(
        functools.partial(restore_kernel, count),
        grid=(rows // block,),
        in_specs=[pl.BlockSpec((1, rows), lambda i: (0, 0))]
        + [pl.BlockSpec((rows, width), lambda i: (0, 0))] * count,
        out_specs=[pl.BlockSpec((block, width), lambda i: (i, 0))] * count,
        out_shape=[jax.ShapeDtypeStruct((rows, width), BF16)] * count,
        compiler_params=pltpu.CompilerParams(vmem_limit_bytes=VMEM_LIMIT),
    )(loc_row, *arrays)


def shards(
    tokens,
    cotangent,
    dealing,
    segments,
    w_query,
    w_key,
    w_value,
    b_query,
    b_value,
    w_out,
    b_out,
    gain_one,
    shift_one,
    w_up,
    b_up,
    w_down,
    b_down,
    gain_two,
    shift_two,
):
    nd, nz = lax.axis_size("pair") * 2, lax.axis_size("tensor")
    rows, width = tokens.shape
    gpp = nd // 4
    per = rows // nd
    part = rows // 4
    slab = w_query.shape[0]
    cols = w_query.shape[1]
    heads = cols // HEAD_DIM
    ff = w_up.shape[1]
    d, z = place()
    t = d % 4
    sds = jax.ShapeDtypeStruct
    dma = pltpu.SemaphoreType.DMA

    core = lax.axis_index("core")
    swap = [(0, 1), (1, 0)]

    def pick(array, index, axis=0):
        return lax.dynamic_index_in_dim(array, index, axis, keepdims=False)

    half, mid = ff // 2, cols // 2
    down_t, out_t = w_down.T, w_out.T
    pieces = jnp.stack(
        [
            jnp.concatenate(
                [
                    w_up[:, h * half : (h + 1) * half],
                    down_t[:, h * half : (h + 1) * half],
                    out_t[:, h * mid : (h + 1) * mid],
                ],
                axis=1,
            )
            for h in range(2)
        ]
    ).astype(BF16)
    got_piece = lax.ppermute(pick(pieces, 1 - core), "core", swap)
    kept = pick(pieces, core)
    shard = jnp.concatenate(
        [jnp.where(core == 0, kept, got_piece), jnp.where(core == 0, got_piece, kept)]
    )
    own_w = lax.all_gather(shard, ("tensor", "pair"), axis=0, tiled=True)
    own_w = own_w.reshape(nz, width, 2 * half + mid)

    pad = 16 - rows // 128
    meta = jnp.concatenate(
        [
            jnp.pad(dealing.reshape(rows // 128, 128), ((0, pad), (0, 0)), constant_values=-1),
            jnp.pad(segments.reshape(rows // 128, 128), ((0, pad), (0, 0))),
        ]
    )
    bias = jnp.concatenate([b_query, b_value, b_up]).reshape(-1, 128)
    bias_rows = bias.shape[0]
    bias = jnp.pad(bias, ((0, -bias_rows % 8), (0, 0)))
    n_meta = nd - 1 + nz - 1
    meta_all, bias_all = comm_call(
        functools.partial(meta_kernel, nd, nz),
        [sds((nd, 32, 128), jnp.int32), sds((nz,) + bias.shape, F32)],
        [dma((n_meta,)), dma((n_meta,))],
        0,
        (meta, bias),
    )
    bias_all = bias_all[:, :bias_rows].reshape(nz, bias_rows * 128)
    own_bias = lax.dynamic_index_in_dim(bias_all, t, 0, keepdims=False)
    bq, bv = own_bias[:cols], own_bias[cols : 2 * cols]
    bu = bias_all[:, 2 * cols :].reshape(nz, 2, half)
    bu = jnp.where(core == 0, bu, bu[:, ::-1])

    loc_all, seg_in = pl.pallas_call(
        functools.partial(index_kernel, nd, gpp, rows),
        in_specs=[vmem_spec()],
        out_specs=[vmem_spec()] * 2,
        out_shape=[sds((nd, per, 1), jnp.int32), sds((nd, per, 1), jnp.int32)],
        compiler_params=pltpu.CompilerParams(vmem_limit_bytes=VMEM_LIMIT),
    )(meta_all)
    send_tok, send_cot = pl.pallas_call(
        functools.partial(gather_kernel, nd, gpp, rows),
        in_specs=[vmem_spec()] * 3,
        out_specs=[vmem_spec()] * 2,
        out_shape=[sds((gpp, per, width), BF16)] * 2,
        compiler_params=pltpu.CompilerParams(vmem_limit_bytes=VMEM_LIMIT),
    )(loc_all, tokens, cotangent)
    wqkv_shard = jnp.concatenate([w_query, w_key, w_value], axis=1).astype(BF16)
    n_disp = nd + max(nd, gpp * nz) + max(gpp, nd // 4)
    x_in, cot_in, wqkv = comm_call(
        functools.partial(dispatch_kernel, nd, nz, gpp),
        [sds((nd, per, width), BF16), sds((nd // 4, per, width), BF16), sds((nd, slab, 3 * cols), BF16)],
        [dma((n_disp,)), dma((n_disp,)), dma((3,))],
        1,
        (send_tok, send_cot, wqkv_shard),
    )
    x_in = x_in.reshape(rows, width)
    wqkv = wqkv.reshape(width, 3 * cols)
    seg_col = seg_in.reshape(rows, 1)
    seg_row = seg_in.reshape(1, rows)

    qkv = jnp.dot(x_in, wqkv, preferred_element_type=F32)
    scale = jnp.where(jnp.arange(3 * cols) < cols, 0.125, 1.0)
    qkv = ((qkv + jnp.concatenate([bq, jnp.zeros_like(bq), bv])) * scale).astype(BF16)
    mixed, lse = attend(qkv, seg_col, seg_row, heads, 256)

    quad = [dma((4,)), dma((4,))]
    mixed_in, oth_w = comm_call(
        quad_kernel,
        [sds((4, part, cols), BF16), sds(own_w.shape, BF16)],
        quad,
        2,
        (mixed.reshape(4, part, cols), own_w),
        in_place=1,
    )
    residual = lax.dynamic_slice_in_dim(x_in, t * part, part, 0)
    zero = jnp.zeros_like(b_out)
    params = jnp.stack([b_out, gain_one, shift_one, b_down, gain_two, shift_two, zero, zero])
    result, grad_attn_in, grad_mixed, dw_own, dw_oth, ubias_grad, sums = rowwise(
        residual, mixed_in, cot_in.reshape(part, width), own_w, oth_w, bu, params
    )
    ubias_grad = jnp.where(core == 0, ubias_grad, ubias_grad[:, ::-1])
    grad_in_mixed, dw_got = comm_call(
        quad_kernel,
        [sds((4, part, cols), BF16), sds(dw_oth.shape, BF16)],
        quad,
        3,
        (grad_mixed, dw_oth),
        in_place=1,
    )
    w_grads = lax.psum_scatter(
        (dw_own + dw_got).reshape(nz * width, 2 * half + mid),
        ("tensor", "pair"),
        scatter_dimension=0,
        tiled=True,
    ).reshape(2, slab, 2 * half + mid)
    g_kept = pick(w_grads, core).astype(F32)
    g_got = lax.ppermute(pick(w_grads, 1 - core), "core", swap).astype(F32)
    g_low, g_high = jnp.where(core == 0, g_kept, g_got), jnp.where(core == 0, g_got, g_kept)
    up_grad = jnp.concatenate([g_low[:, :half], g_high[:, :half]], axis=1)
    down_grad = jnp.concatenate([g_low[:, half : 2 * half], g_high[:, half : 2 * half]], axis=1).T
    out_grad = jnp.concatenate([g_low[:, 2 * half :], g_high[:, 2 * half :]], axis=1).T

    grad_in_mixed = grad_in_mixed.reshape(rows, cols)
    dq, dkv = attend_back(qkv, grad_in_mixed, lse, seg_col, seg_row, heads, 256)
    dqkv = jnp.concatenate([dq, dkv], axis=1)
    bias_sums = jnp.sum(dqkv, axis=0, dtype=F32)
    back_part = jnp.einsum("rc,dc->rd", dqkv, wqkv, preferred_element_type=F32).astype(BF16)
    dw = jnp.einsum("rd,rc->dc", x_in, dqkv, preferred_element_type=F32).astype(BF16)
    back_part = back_part.reshape(2, 2, part, width)
    part_got = lax.ppermute(pick(back_part, 1 - core, 1), "core", swap)
    part_sum = pick(back_part, core, 1).astype(F32) + part_got.astype(F32)
    mine = (jnp.arange(nz) == t)[:, None]
    vec = jnp.concatenate(
        [
            jnp.where(mine, bias_sums[:cols], 0.0).reshape(-1),
            jnp.where(mine, bias_sums[2 * cols :], 0.0).reshape(-1),
            sums[:6].reshape(-1),
            ubias_grad.reshape(-1),
        ]
    ).reshape(-1, 128)
    n_back = gpp + nd
    part_in, vec_in, dw_in = comm_call(
        functools.partial(back_kernel, nd, gpp),
        [
            sds((part, width), BF16),
            sds((nd,) + vec.shape, F32),
            sds((gpp, 4, slab, 3 * cols), BF16),
        ],
        [dma((n_back,)), dma((n_back,))],
        4,
        (part_sum.astype(BF16), vec, dw.reshape(gpp, 4, slab, 3 * cols)),
    )
    grad_in = grad_attn_in + pick(part_sum, t // 2) + part_in.astype(F32)
    dw_low = jnp.sum(dw_in, axis=0, dtype=F32).astype(BF16)
    vec_plane = jnp.sum(vec_in, axis=0)
    quarter = nd // 4
    block = (quarter, per, width)
    got, got_grad, vec_z, dw_z = comm_call(
        functools.partial(combine_kernel, nd, nz, gpp, 2),
        [sds((nz, gpp, per, width), BF16)] * 2
        + [sds((nz,) + vec.shape, F32), sds((nz, slab, 3 * cols), BF16)],
        [
            dma((2, quarter)),
            dma((2, gpp)),
            dma((2, nz)),
            dma((2, nz)),
            dma((2, nz)),
            dma((2, nz)),
            dma((nz,)),
            dma((nz,)),
            dma((4,)),
            dma((nz,)),
            dma((3,)),
        ],
        5,
        (result.reshape(block), grad_in.astype(BF16).reshape(block), vec_plane, dw_low),
    )
    dw_sum = jnp.sum(dw_z, axis=0, dtype=F32)
    layer_out, grad_tokens = restore(
        loc_all.reshape(1, rows), (got.reshape(rows, width), got_grad.reshape(rows, width)), 256
    )
    vec_all = jnp.sum(vec_z, axis=0).reshape(-1)
    q_all, v_all = vec_all[:width].reshape(nz, cols), vec_all[width : 2 * width].reshape(nz, cols)
    rest = vec_all[2 * width : 8 * width].reshape(6, width)
    u_all = vec_all[8 * width :].reshape(nz, ff)

    return (
        layer_out,
        grad_tokens,
        dw_sum[:, :cols],
        dw_sum[:, cols : 2 * cols],
        dw_sum[:, 2 * cols :],
        pick(q_all, z),
        pick(v_all, z),
        out_grad,
        rest[0],
        rest[1],
        rest[2],
        up_grad,
        pick(u_all, z),
        down_grad,
        rest[3],
        rest[4],
        rest[5],
    )


def solution(mesh):
    split = (mesh.shape["dp"] // 2, 2, mesh.shape["tensor"])
    mesh = jax.sharding.Mesh(mesh.devices.reshape(split), ("pair", "core", "tensor"))
    in_specs = (
        P(DP, None),
        P(DP, None),
        P(DP),
        P(DP, None),
        P(DP, "tensor"),
        P(DP, "tensor"),
        P(DP, "tensor"),
        P("tensor"),
        P("tensor"),
        P("tensor", DP),
        P(),
        P(),
        P(),
        P(DP, "tensor"),
        P("tensor"),
        P("tensor", DP),
        P(),
        P(),
        P(),
    )
    out_specs = (
        P(DP, None),
        P(DP, None),
        P(DP, "tensor"),
        P(DP, "tensor"),
        P(DP, "tensor"),
        P("tensor"),
        P("tensor"),
        P("tensor", DP),
        P(),
        P(),
        P(),
        P(DP, "tensor"),
        P("tensor"),
        P("tensor", DP),
        P(),
        P(),
        P(),
    )
    return jax.shard_map(shards, mesh=mesh, in_specs=in_specs, out_specs=out_specs, check_vma=False)
```
